256 devices in a mesh: row: 16 (over y, x_lo, core), col: 16 (over x_hi, z).
Axes of the slice: x: 4 (x_hi: 2, x_lo: 2; x = x_hi * 2 + x_lo), y: 4, z: 8, core: 2. Of those that a mesh axis runs over, the one named last changes fastest.
Arguments:
- amplitudes: float32 [32, 4, 512, 512], P('row', None, 'col'), may hold values from -6 to 6
- integrals: float32 [4, 512, 32, 512], P(None, 'row', 'col'), may hold values from -0.125 to 0.125
- occ_energy: float32 [32], replicated, may hold values from -1.5 to -0.3
- vir_energy: float32 [512], replicated, may hold values from 0.2 to 3
Outputs:
- update: float32 [32, 32, 512, 512], P('row', None, 'col')
The draws below stay inside these ranges and needn't reach their ends.
All inputs are finite; a program needn't handle non-finite values.
Results may differ from the reference program's by a relative error of at most 0.00007.
Values sent between devices are 32-bit elements; how exact they have to be, the bound alone decides.
A program may use at most 64 MiB of HBM per device.

```python
import jax
import jax.numpy as jnp
from jax import lax

O = 32
V = 512
KOCC = 4


def shard_levels(stream_key, shape, cuts, low, top_value):
    gain = 1.0
    for position, parts in cuts:
        steps = jax.random.uniform(jax.random.fold_in(jax.random.fold_in(stream_key, 6), position), (parts,), jnp.float32, low / len(cuts), top_value / len(cuts))
        gain = gain * jnp.repeat(jnp.exp(steps), shape[position] // parts).reshape((-1,) + (1,) * (len(shape) - 1 - position))
    return gain


def centred(stream_key, shape, spread, reach, cuts=(), kind=jnp.bfloat16):
    values = jax.random.normal(stream_key, shape, jnp.float32) * spread
    if len(cuts) > 0:
        values = shard_levels(stream_key, shape, cuts, -0.22, 0.18) * values
    return jnp.clip(values, min=-reach, max=reach).astype(kind)


def setup_inputs(seed: int = 0) -> dict:
    arg_keys = jax.random.split(jax.random.key(seed), 5)
    amplitudes = centred(arg_keys[0], (O, KOCC, V, V), 1.0, 6.0, ((0, 16), (2, 16)), jnp.float32)
    integrals = centred(arg_keys[1], (KOCC, V, O, V), (KOCC * V) ** -0.5, 0.125, ((1, 16), (2, 16)), jnp.float32)
    occ_energy = jnp.clip(jax.random.uniform(arg_keys[2], (O,), jnp.float32, -1.5, -0.3), -1.5, -0.3)
    vir_energy = jnp.clip(jax.random.uniform(arg_keys[3], (V,), jnp.float32, 0.2, 3.0), 0.2, 3.0)
    return dict(amplitudes=amplitudes, integrals=integrals, occ_energy=occ_energy, vir_energy=vir_energy)


def reference(amplitudes, integrals, occ_energy, vir_energy):
    def one_row(index):
        cycle = jnp.einsum('kac,kcjb->jab', amplitudes[index], integrals, precision=lax.Precision.HIGHEST)
        denom = occ_energy[index] + occ_energy[:, None, None] - vir_energy[None, :, None] - vir_energy[None, None, :]
        return cycle / denom

    return lax.map(one_row, jnp.arange(O, dtype=jnp.int32))
```

```python
import jax
import jax.numpy as jnp
from jax import lax
from jax.experimental import pallas as pl
from jax.experimental.pallas import tpu as pltpu
from jax.sharding import PartitionSpec as P

MESH = pl.DeviceIdType.MESH
NZ = 8


def place(x, y, z, core):
    return (y * 4 + (x % 2) * 2 + core, (x // 2) * NZ + z)


def kernel(t_hbm, w_hbm, out, w_raw, w_src, w_buf, t_buf, t_hi, t_lo, acc,
           load_sem, pre_send, pre_recv, ring_send, ring_recv, part_send, part_recv,
           t_send, t_recv, c_send, c_recv, own_sem):
    row, col = lax.axis_index("row"), lax.axis_index("col")
    y, xl, core = row // 4, (row // 2) % 2, row % 2
    xh, z = col // NZ, col % NZ
    x = xh * 2 + xl
    par = y % 2
    s = y * 2 + xl
    y_pair = y + 1 - 2 * par

    def flip(v, bits, width):
        for b in range(width):
            if (bits >> b) & 1:
                v = v + (1 << b) * (1 - 2 * ((v // (1 << b)) % 2))
        return v

    def remote(src, dst, send, recv, device):
        return pltpu.make_async_remote_copy(src, dst, send, recv, device_id=device, device_id_type=MESH)

    pre_dev = {}
    for e in range(1, 8):
        se = flip(s, e, 3)
        pre_dev[e] = (se // 2, se % 2)
    group = [(dx, dp) for dx in (1, 3, 0, 2) for dp in (0, 1) if (dx, dp) != (0, 0)]
    z_next = {0: (z + 1) % NZ, 1: (z + NZ - 1) % NZ}
    partner = place(x, y, z, 1 - core)

    def group_dev(dx, dp):
        return place((x + dx) % 4, y_pair if dp else y, z, core)

    everyone = [place(xh * 2 + pre_dev[e][1], pre_dev[e][0], z, core) for e in pre_dev]
    everyone += [group_dev(dx, dp) for dx, dp in group]
    everyone += [place(x, y, z_next[0], core), place(x, y, z_next[1], core), partner]

    load_w = pltpu.make_async_copy(w_hbm, w_raw, load_sem.at[0])
    load_w.start()
    own_u = x * 2 + par
    load_t = pltpu.make_async_copy(t_hbm, t_buf.at[own_u], load_sem.at[1])
    load_t.start()

    barrier = pltpu.get_barrier_semaphore()
    for d in everyone:
        pl.semaphore_signal(barrier, inc=1, device_id=d, device_id_type=MESH)

    load_w.wait()
    for k in range(4):
        for jj in range(2):
            for bh in range(2):
                w_src[jj, bh, k] = w_raw[k, :, jj, bh * 256:bh * 256 + 256]
    pl.semaphore_wait(barrier, len(everyone))

    own_w = pltpu.make_async_copy(w_src.at[xl, par], w_buf.at[z, :, s, core], load_sem.at[2])
    own_w.start()
    pending = []

    def start(cp):
        cp.start()
        pending.append(cp)

    def pre(e):
        ye, xe = pre_dev[e]
        return remote(w_src.at[xe, ye % 2], w_buf.at[z, :, s, core], pre_send.at[e], pre_recv.at[e],
                      place(xh * 2 + xe, ye, z, core))

    def pre_wait(e):
        ye, xe = pre_dev[e]
        view = w_buf.at[z, :, ye * 2 + xe, core]
        remote(view, view, pre_send.at[e], pre_recv.at[e], partner).wait_recv()

    for e in (1, 2, 3, 6, 7, 4, 5):
        start(pre(e))

    xm, xp = (x + 3) % 4, (x + 1) % 4
    dev_y, dev_xp, dev_xm = group_dev(0, 1), group_dev(1, 0), group_dev(3, 0)

    def t_view(u, half):
        return t_buf.at[u] if half is None else t_buf.at[u, half]

    def t_copy(u, half, k, device, src=None):
        v = t_view(u, half)
        start(remote(v if src is None else src, v, t_send.at[k], t_recv.at[k], device))

    def t_wait(u, half, k):
        v = t_view(u, half)
        remote(v, v, t_send.at[k], t_recv.at[k], partner).wait_recv()

    t_copy(own_u, None, 0, dev_y, t_hbm)
    t_copy(own_u, None, 1, dev_xp, t_hbm)
    t_copy(own_u, None, 3, dev_xm, t_hbm)

    chunks = [(s, 1), (flip(s, 1, 3), 1), ((flip(s, 2, 3) // 2) * 2, 2), ((flip(s, 4, 3) // 4) * 4, 4)]
    fresh = {0: (), 1: (1,), 2: (2, 3), 3: (4, 5, 6, 7)}

    def w_view(zs, ch, which):
        base, size = chunks[ch]
        return w_buf.at[zs, :, pl.ds(base, size), which]

    def slice_at(d, n):
        return (z + NZ - n) % NZ if d == 0 else (z + n) % NZ

    def ring_wait(d, n, ch):
        v = w_view(slice_at(d, n), ch, core)
        remote(v, v, ring_send.at[d, n - 1, ch], ring_recv.at[d, n - 1, ch], partner).wait_recv()

    def ring_forward(d, n, ch):
        v = w_view(slice_at(d, n), ch, core)
        start(remote(v, v, ring_send.at[d, n, ch], ring_recv.at[d, n, ch], place(x, y, z_next[d], core)))

    def slot_of(d, n):
        return 0 if n == 0 else 7 if n == 4 else 2 * n - 1 + d

    def to_partner(d, n, ch):
        v = w_view(slice_at(d, n), ch, core)
        k = slot_of(d, n)
        start(remote(v, v, part_send.at[k, ch], part_recv.at[k, ch], partner))

    def partner_wait(d, n):
        k = slot_of(d, n)
        for ch in range(4):
            v = w_view(slice_at(d, n), ch, 1 - core)
            remote(v, v, part_send.at[k, ch], part_recv.at[k, ch], partner).wait_recv()

    def goes_on(d, n, ch):
        return n < 3 or (n == 3 and ((ch < 3) if d == 0 else (ch == 3)))

    def relay(n):
        for ch in range(4):
            if n == 0:
                for e in fresh[ch]:
                    pre_wait(e)
            for d in range(2):
                if n > 0:
                    ring_wait(d, n, ch)
                if goes_on(d, n, ch):
                    ring_forward(d, n, ch)
                if n > 0 or d == 0:
                    to_partner(d, n, ch)

    def convert(u):
        for i in range(2):
            for k in range(4):
                v = t_buf[u, i, k]
                hi = v.astype(jnp.bfloat16)
                rows = pl.ds(pl.multiple_of(u * 64 + i * 32, 32), 32)
                t_hi[k, rows, :] = hi
                t_lo[k, rows, :] = (v - hi.astype(jnp.float32)).astype(jnp.bfloat16)

    def compute(d, n):
        zs = slice_at(d, n)
        k_slot = slot_of(d, n)

        def step(k, carry):
            w = w_buf[zs, k].reshape(512, 256)
            w_hi = w.astype(jnp.bfloat16)
            w_lo = (w - w_hi.astype(jnp.float32)).astype(jnp.bfloat16)
            p = jnp.dot(t_hi[k], w_hi, preferred_element_type=jnp.float32)
            p += jnp.dot(t_lo[k], w_hi, preferred_element_type=jnp.float32)
            p += jnp.dot(t_hi[k], w_lo, preferred_element_type=jnp.float32)
            p = p.reshape(8, 2, 32, 256)

            @pl.when(k == 0)
            def _():
                acc[zs] = p

            @pl.when(k > 0)
            def _():
                acc[zs] += p

            return carry

        lax.fori_loop(0, 4, step, 0)
        j = 2 * (xh * NZ + zs) + xl
        lanes = pl.ds(pl.multiple_of(par * 256, 256), 256)
        dst = out.at[:, j, :, lanes]
        for q, (dx, dp) in enumerate(group):
            u = ((x + dx) % 4) * 2 + ((1 - par) if dp else par)
            start(remote(acc.at[zs, u], dst, c_send.at[q, k_slot], c_recv.at[q, k_slot], group_dev(dx, dp)))
        own = pltpu.make_async_copy(acc.at[zs, own_u], dst, own_sem.at[k_slot])
        own.start()
        locals_.append(own)

    locals_ = []
    own_w.wait()
    relay(0)

    um, up = xm * 2 + par, xp * 2 + par
    uy, umy, upy = x * 2 + 1 - par, xm * 2 + 1 - par, xp * 2 + 1 - par
    u2, u2y = ((x + 2) % 4) * 2 + par, ((x + 2) % 4) * 2 + 1 - par
    t_wait(um, None, 1)
    t_copy(um, 0, 5, dev_xp)
    t_wait(up, None, 3)
    t_copy(up, 1, 7, dev_xm)
    t_wait(uy, None, 0)
    t_copy(uy, None, 2, dev_xp)
    t_copy(uy, None, 4, dev_xm)
    load_t.wait()
    relay(1)
    t_wait(umy, None, 2)
    t_copy(umy, 0, 6, dev_xp)
    t_wait(upy, None, 4)
    t_copy(upy, 1, 8, dev_xm)
    t_wait(u2, 0, 5)
    t_wait(u2, 1, 7)
    t_wait(u2y, 0, 6)
    t_wait(u2y, 1, 8)
    lax.fori_loop(0, 8, lambda u, c: (convert(u), c)[1], 0)
    partner_wait(0, 0)
    compute(0, 0)
    for n in (1, 2, 3):
        if n > 1:
            relay(n)
        for d in range(2):
            partner_wait(d, n)
            compute(d, n)
    for ch in range(4):
        d = 0 if ch < 3 else 1
        ring_wait(d, 4, ch)
        to_partner(d, 4, ch)
    partner_wait(0, 4)
    compute(0, 4)

    for cp in pending:
        cp.wait_send()
    for cp in locals_:
        cp.wait()
    for q in range(7):
        for k in range(8):
            v = out.at[:, k, :, pl.ds(0, 256)]
            remote(v, v, c_send.at[q, k], c_recv.at[q, k], partner).wait_recv()


def body(amplitudes, integrals, occ_energy, vir_energy):
    dma = pltpu.SemaphoreType.DMA
    f32, bf16 = jnp.float32, jnp.bfloat16
    cycle = pl.pallas_call(
        kernel,
        out_shape=jax.ShapeDtypeStruct((2, 32, 32, 512), f32),
        in_specs=[pl.BlockSpec(memory_space=pl.ANY)] * 2,
        out_specs=pl.BlockSpec(memory_space=pl.ANY),
        scratch_shapes=[
            pltpu.VMEM((4, 32, 2, 512), f32),
            pltpu.VMEM((2, 2, 4, 32, 256), f32),
            pltpu.VMEM((8, 4, 8, 2, 32, 256), f32),
            pltpu.VMEM((8, 2, 4, 32, 512), f32),
            pltpu.VMEM((4, 512, 512), bf16),
            pltpu.VMEM((4, 512, 512), bf16),
            pltpu.VMEM((8, 8, 2, 32, 256), f32),
            dma((3,)), dma((8,)), dma((8,)), dma((2, 4, 4)), dma((2, 4, 4)), dma((8, 4)), dma((8, 4)),
            dma((9,)), dma((9,)), dma((7, 8)), dma((7, 8)), dma((8,)),
        ],
        compiler_params=pltpu.CompilerParams(
            collective_id=0, has_side_effects=True, vmem_limit_bytes=60 * 2**20
        ),
    )(amplitudes, integrals)
    rows_i, a_local = cycle.shape[0], cycle.shape[2]
    occ_local = lax.dynamic_slice_in_dim(occ_energy, lax.axis_index("row") * rows_i, rows_i, 0)
    vir_local = lax.dynamic_slice_in_dim(vir_energy, lax.axis_index("col") * a_local, a_local, 0)
    denom = (
        occ_local[:, None, None, None]
        + occ_energy[None, :, None, None]
        - vir_local[None, None, :, None]
        - vir_energy[None, None, None, :]
    )
    return cycle / denom


def solution(mesh):
    return jax.shard_map(
        body,
        mesh=mesh,
        in_specs=(P("row", None, "col", None), P(None, "row", "col", None), P(), P()),
        out_specs=P("row", None, "col", None),
        check_vma=False,
    )
```

```python
import jax
import jax.numpy as jnp
from jax import lax
from jax.experimental import pallas as pl
from jax.experimental.pallas import tpu as pltpu
from jax.sharding import PartitionSpec as P

MESH = pl.DeviceIdType.MESH
NZ = 8
NEAR = ((0, 0), (1, 1), (1, 3), (1, 0), (0, 2), (0, 1), (0, 3), (3, 0))


def place(x, y, z, core):
    return (y * 4 + (x % 2) * 2 + core, (x // 2) * NZ + z)


def flip(v, bits):
    for b in range(3):
        if (bits >> b) & 1:
            v = v + (1 << b) * (1 - 2 * ((v // (1 << b)) % 2))
    return v


def kernel(t_hbm, w_hbm, occ, vir, out, w_raw, w_src, w_buf, t_buf, t_hi, t_lo, acc, vir_a,
           load_sem, pre_send, pre_recv, ring_send, ring_recv, part_send, part_recv,
           t_send, t_recv, c_send, c_recv, own_sem):
    row, col = lax.axis_index("row"), lax.axis_index("col")
    y, xl, core = row // 4, (row // 2) % 2, row % 2
    xh, z = col // NZ, col % NZ
    x = xh * 2 + xl
    s = y * 2 + xl
    far = y // 2
    from_xh = xh + far * (1 - 2 * xh)
    half = y % 2
    z_next = ((z + 1) % NZ, (z + NZ - 1) % NZ)
    partner = place(x, y, z, 1 - core)
    pending, locals_ = [], []

    def remote(src, dst, send, recv, device):
        return pltpu.make_async_remote_copy(src, dst, send, recv, device_id=device, device_id_type=MESH)

    def start(cp):
        cp.start()
        pending.append(cp)

    def arrived(view, recv):
        remote(view, view, load_sem.at[0], recv, partner).wait_recv()

    load_w = pltpu.make_async_copy(w_hbm, w_raw, load_sem.at[0])
    load_w.start()
    load_t = pltpu.make_async_copy(t_hbm, t_buf.at[0], load_sem.at[1])
    load_t.start()

    barrier = pltpu.get_barrier_semaphore()
    everyone = [place((x + dx) % 4, (y + dy) % 4, z, core)
                for dx in range(4) for dy in range(4) if (dx, dy) != (0, 0)]
    everyone += [place(x, y, z_next[0], core), place(x, y, z_next[1], core), partner]
    for d in everyone:
        pl.semaphore_signal(barrier, inc=1, device_id=d, device_id_type=MESH)

    load_w.wait()
    for k in range(4):
        for jj in range(2):
            for bh in range(2):
                w_src[jj, bh, k] = w_raw[k, :, jj, bh * 256:bh * 256 + 256]
    pl.semaphore_wait(barrier, len(everyone))

    def pre(e):
        se = flip(s, e)
        ye, xe = se // 2, se % 2
        xhe = xh + (ye // 2) * (1 - 2 * xh)
        return remote(w_src.at[xe, ye % 2], w_buf.at[z, :, s, core], pre_send.at[e], pre_recv.at[e],
                      place(xhe * 2 + xe, ye, z, core))

    def pre_wait(e, se):
        arrived(w_buf.at[z, :, se, core], pre_recv.at[e])

    own_w = pltpu.make_async_copy(w_src.at[xl, half], w_buf.at[z, :, s, core], pre_recv.at[0])
    first = pre(0)

    @pl.when(far == 0)
    def _():
        own_w.start()

    start(pre(1))

    @pl.when(far == 1)
    def _():
        first.start()

    for e in (2, 3, 6, 7, 4, 5):
        start(pre(e))

    for r, (dx, dy) in enumerate(NEAR):
        if r > 0:
            start(remote(t_hbm, t_buf.at[r], t_send.at[r], t_recv.at[r],
                         place((x + dx) % 4, (y + dy) % 4, z, core)))

    s0 = flip(s, 1) * far + s * (1 - far)
    chunks = [(s0, 1), (flip(s0, 1), 1)] + [((flip(s, e) // 2) * 2, 2) for e in (2, 6, 4)]

    def w_view(zs, ch, which):
        base, size = chunks[ch]
        return w_buf.at[zs, :, pl.ds(base, size), which]

    def slice_at(d, n):
        return (z + NZ - n) % NZ if d == 0 else (z + n) % NZ

    def slot_of(d, n):
        return 0 if n == 0 else 7 if n == 4 else 2 * n - 1 + d

    def goes_on(d, n, ch):
        return n < 3 or (n == 3 and ((ch < 3) if d == 0 else (ch >= 3)))

    def relay(n, ch):
        if n == 0:
            if ch == 0:
                pre_wait(far, s0)
            elif ch == 1:
                pre_wait(1 - far, flip(s0, 1))
            else:
                e = (2, 6, 4)[ch - 2]
                pre_wait(e, flip(s, e))
                pre_wait(e + 1, flip(s, e + 1))
        for d in range(2):
            if n == 4 and d != (0 if ch < 3 else 1):
                continue
            v = w_view(slice_at(d, n), ch, core)
            if n > 0:
                arrived(v, ring_recv.at[d, n - 1, ch])
            if goes_on(d, n, ch):
                start(remote(v, v, ring_send.at[d, n, ch], ring_recv.at[d, n, ch],
                             place(x, y, z_next[d], core)))
            if n > 0 or d == 0:
                k = slot_of(d, n)
                start(remote(v, v, part_send.at[k, ch], part_recv.at[k, ch], partner))

    def partner_wait(d, n):
        for ch in range(5):
            arrived(w_view(slice_at(d, n), ch, 1 - core), part_recv.at[slot_of(d, n), ch])

    def convert(r):
        for i in range(2):
            for k in range(4):
                v = t_buf[r, i, k]
                hi = v.astype(jnp.bfloat16)
                rows = pl.ds(r * 64 + i * 32, 32)
                t_hi[k, rows, :] = hi
                t_lo[k, rows, :] = (v - hi.astype(jnp.float32)).astype(jnp.bfloat16)

    lane = lax.broadcasted_iota(jnp.int32, (32, 512), 1)
    sub = lax.broadcasted_iota(jnp.int32, (32, 512), 0)
    vir_row = jnp.broadcast_to(vir[...], (32, 512))
    for h in range(2):
        picked = jnp.where(lane == sub + (h * NZ + z) * 32, vir_row, 0.0)
        vir_a[h] = jnp.broadcast_to(jnp.sum(picked, axis=1, keepdims=True), (32, 128))

    def compute(d, n):
        zs = slice_at(d, n)
        k_slot = slot_of(d, n)
        partner_wait(d, n)

        def step(k, carry):
            w = w_buf[zs, k].reshape(512, 256)
            w_hi = w.astype(jnp.bfloat16)
            w_lo = (w - w_hi.astype(jnp.float32)).astype(jnp.bfloat16)
            p = jnp.dot(t_hi[k], w_hi, preferred_element_type=jnp.float32)
            p += jnp.dot(t_lo[k], w_hi, preferred_element_type=jnp.float32)
            p += jnp.dot(t_hi[k], w_lo, preferred_element_type=jnp.float32)
            p = p.reshape(8, 2, 32, 256)

            @pl.when(k == 0)
            def _():
                acc[zs] = p

            @pl.when(k > 0)
            def _():
                acc[zs] += p

            return carry

        lax.fori_loop(0, 4, step, 0)
        j = 2 * (from_xh * NZ + zs) + xl
        lanes = pl.ds(pl.multiple_of(half * 256, 256), 256)
        dst = out.at[:, j, :, lanes]
        vir_b = vir[:, lanes]
        occ_j = occ[j]
        order = list(range(1, 8)) + [0]
        for r in order:
            dx, dy = NEAR[r]
            xo, yo = (x + 4 - dx) % 4, (y + 4 - dy) % 4
            column = vir_a[xo // 2]
            column = jnp.concatenate([column, column], axis=1)
            for i in range(2):
                occ_i = occ[(yo * 4 + (xo % 2) * 2 + core) * 2 + i]
                denom = ((occ_i + occ_j) - column) - vir_b
                acc[zs, r, i] = acc[zs, r, i] / denom
        for r in order:
            dx, dy = NEAR[r]
            if r > 0:
                start(remote(acc.at[zs, r], dst, c_send.at[r, k_slot], c_recv.at[r, k_slot],
                             place((x + 4 - dx) % 4, (y + 4 - dy) % 4, z, core)))
            else:
                own = pltpu.make_async_copy(acc.at[zs, r], dst, own_sem.at[k_slot])
                own.start()
                locals_.append(own)

    def relays(n, *chs):
        for ch in chs:
            relay(n, ch)

    def t_ready(*rs):
        for r in rs:
            arrived(t_buf.at[r], t_recv.at[r])
            convert(r)

    relays(0, 0, 1, 2, 3, 4)
    load_t.wait()
    convert(0)
    relays(1, 0, 1, 2, 3, 4)
    t_ready(1, 2, 3)
    relays(2, 0, 1, 2)
    t_ready(4, 5, 6, 7)
    relays(2, 3)
    compute(0, 0)
    relays(2, 4)
    compute(0, 1)
    compute(1, 1)
    relays(3, 0)
    compute(0, 2)
    relays(3, 1)
    compute(1, 2)
    relays(3, 2, 3, 4)
    compute(0, 3)
    compute(1, 3)
    relays(4, 0, 1, 3, 2, 4)
    compute(0, 4)

    for cp in pending:
        cp.wait_send()

    @pl.when(far == 1)
    def _():
        first.wait_send()

    for cp in locals_:
        cp.wait()
    for r in range(1, 8):
        for k in range(8):
            arrived(out.at[:, k, :, pl.ds(0, 256)], c_recv.at[r, k])


def body(amplitudes, integrals, occ_energy, vir_energy):
    dma = pltpu.SemaphoreType.DMA
    f32, bf16 = jnp.float32, jnp.bfloat16
    hbm = pl.BlockSpec(memory_space=pl.ANY)
    return pl.pallas_call(
        kernel,
        out_shape=jax.ShapeDtypeStruct((2, 32, 32, 512), f32),
        in_specs=[hbm, hbm, pl.BlockSpec(memory_space=pltpu.SMEM), pl.BlockSpec(memory_space=pltpu.VMEM)],
        out_specs=OUT_SPEC,
        scratch_shapes=[
            pltpu.VMEM((4, 32, 2, 512), f32),
            pltpu.VMEM((2, 2, 4, 32, 256), f32),
            pltpu.VMEM((8, 4, 8, 2, 32, 256), f32),
            pltpu.VMEM((8, 2, 4, 32, 512), f32),
            pltpu.VMEM((4, 512, 512), bf16),
            pltpu.VMEM((4, 512, 512), bf16),
            pltpu.VMEM((8, 8, 2, 32, 256), f32),
            pltpu.VMEM((2, 32, 128), f32),
            dma((2,)), dma((8,)), dma((8,)), dma((2, 4, 5)), dma((2, 4, 5)), dma((8, 5)), dma((8, 5)),
            dma((8,)), dma((8,)), dma((8, 8)), dma((8, 8)), dma((8,)),
        ],
        compiler_params=pltpu.CompilerParams(
            collective_id=0, has_side_effects=True, vmem_limit_bytes=60 * 2**20
        ),
    )(amplitudes, integrals, occ_energy, vir_energy.reshape(1, -1))


OUT_SPEC = pl.BlockSpec(memory_space=pl.ANY)


def solution(mesh):
    return jax.shard_map(
        body,
        mesh=mesh,
        in_specs=(P("row", None, "col", None), P(None, "row", "col", None), P(), P()),
        out_specs=P("row", None, "col", None),
        check_vma=False,
    )
```

```python
import jax
import jax.numpy as jnp
from jax import lax
from jax.experimental import pallas as pl
from jax.experimental.pallas import tpu as pltpu
from jax.sharding import PartitionSpec as P

MESH = pl.DeviceIdType.MESH
NZ = 8


def place(x, y, z, core):
    return (y * 4 + (x % 2) * 2 + core, (x // 2) * NZ + z)


def flip(v, bits):
    for b in range(3):
        if (bits >> b) & 1:
            v = v + (1 << b) * (1 - 2 * ((v // (1 << b)) % 2))
    return v


def kernel(t_hbm, w_hbm, occ, vir, out, w_raw, w_src, w_buf, t_buf, t_hi, t_lo, acc, vir_a,
           load_sem, pre_send, pre_recv, ring_send, ring_recv, part_send, part_recv,
           t_send, t_recv, c_send, c_recv, own_sem):
    row, col = lax.axis_index("row"), lax.axis_index("col")
    y, xl, core = row // 4, (row // 2) % 2, row % 2
    xh, z = col // NZ, col % NZ
    x = xh * 2 + xl
    s = y * 2 + xl
    block = (y + 2 * xl) % 4
    jj, bh = block // 2, block % 2
    inner, outer = 1 + 2 * xl, 3 - 2 * xl
    THERE = ((0, 0), (outer, 0), (outer, 1), (outer, 3), (2, 0), (inner, 0), (0, 1), (0, 3))
    BACK = ((0, 0), (outer, 0), (outer, 3), (outer, 1), (2, 0), (inner, 0), (0, 3), (0, 1))
    z_next = ((z + 1) % NZ, (z + NZ - 1) % NZ)
    partner = place(x, y, z, 1 - core)
    pending, locals_ = [], []

    def remote(src, dst, send, recv, device):
        return pltpu.make_async_remote_copy(src, dst, send, recv, device_id=device, device_id_type=MESH)

    def start(cp):
        cp.start()
        pending.append(cp)

    def arrived(view, recv):
        remote(view, view, load_sem.at[0], recv, partner).wait_recv()

    load_w = pltpu.make_async_copy(w_hbm, w_raw, load_sem.at[0])
    load_w.start()
    load_t = pltpu.make_async_copy(t_hbm, t_buf.at[0], load_sem.at[1])
    load_t.start()

    barrier = pltpu.get_barrier_semaphore()
    everyone = [place((x + dx) % 4, (y + dy) % 4, z, core)
                for dx in range(4) for dy in range(4) if (dx, dy) != (0, 0)]
    everyone += [place(x, y, z_next[0], core), place(x, y, z_next[1], core), partner]
    for d in everyone:
        pl.semaphore_signal(barrier, inc=1, device_id=d, device_id_type=MESH)

    load_w.wait()
    for k in range(4):
        for b in range(4):
            w_src[b // 2, b % 2, k] = w_raw[k, :, b // 2, (b % 2) * 256:(b % 2) * 256 + 256]
    pl.semaphore_wait(barrier, len(everyone))

    def pre(e):
        se = flip(s, e)
        ye, xe = se // 2, se % 2
        be = (ye + 2 * xe) % 4
        return remote(w_src.at[be // 2, be % 2], w_buf.at[z, :, s, core], pre_send.at[e], pre_recv.at[e],
                      place(xh * 2 + xe, ye, z, core))

    def pre_wait(e):
        arrived(w_buf.at[z, :, flip(s, e), core], pre_recv.at[e])

    own_w = pltpu.make_async_copy(w_src.at[jj, bh], w_buf.at[z, :, s, core], load_sem.at[2])
    own_w.start()

    def send_t(*rs):
        for r in rs:
            dx, dy = THERE[r]
            start(remote(t_hbm, t_buf.at[r], t_send.at[r], t_recv.at[r],
                         place((x + dx) % 4, (y + dy) % 4, z, core)))

    def t_relay(r, dy):
        start(remote(t_buf.at[1], t_buf.at[r], t_send.at[r], t_recv.at[r], place(x, (y + dy) % 4, z, core)))

    chunks = [(s, 1), (flip(s, 1), 1)] + [((flip(s, e) // 2) * 2, 2) for e in (2, 6, 4)]

    def w_view(zs, ch, which):
        base, size = chunks[ch]
        return w_buf.at[zs, :, pl.ds(base, size), which]

    def slice_at(d, n):
        return (z + NZ - n) % NZ if d == 0 else (z + n) % NZ

    def slot_of(d, n):
        return 0 if n == 0 else 7 if n == 4 else 2 * n - 1 + d

    def goes_on(d, n, ch):
        return n < 3 or (n == 3 and ((ch < 3) if d == 0 else (ch >= 3)))

    def relay(n, ch):
        if n == 0:
            for e in ((), (1,), (2, 3), (6, 7), (4, 5))[ch]:
                pre_wait(e)
        for d in range(2):
            if n == 4 and d != (0 if ch < 3 else 1):
                continue
            v = w_view(slice_at(d, n), ch, core)
            if n > 0:
                arrived(v, ring_recv.at[d, n - 1, ch])
            source = v
            if n == 0 and ch == 0:
                source, v = w_src.at[jj, bh], w_buf.at[z, :, s, core]
            if goes_on(d, n, ch):
                start(remote(source, v, ring_send.at[d, n, ch], ring_recv.at[d, n, ch],
                             place(x, y, z_next[d], core)))
            if n > 0 or d == 0:
                k = slot_of(d, n)
                start(remote(source, v, part_send.at[k, ch], part_recv.at[k, ch], partner))

    def partner_wait(d, n):
        for ch in range(5):
            arrived(w_view(slice_at(d, n), ch, 1 - core), part_recv.at[slot_of(d, n), ch])

    def convert(r):
        for i in range(2):
            for k in range(4):
                v = t_buf[r, i, k]
                hi = v.astype(jnp.bfloat16)
                rows = pl.ds(r * 64 + i * 32, 32)
                t_hi[k, rows, :] = hi
                t_lo[k, rows, :] = (v - hi.astype(jnp.float32)).astype(jnp.bfloat16)

    lane = lax.broadcasted_iota(jnp.int32, (32, 512), 1)
    sub = lax.broadcasted_iota(jnp.int32, (32, 512), 0)
    vir_row = jnp.broadcast_to(vir[...], (32, 512))
    for h in range(2):
        picked = jnp.where(lane == sub + (h * NZ + z) * 32, vir_row, 0.0)
        vir_a[h] = jnp.broadcast_to(jnp.sum(picked, axis=1, keepdims=True), (32, 128))

    def compute(d, n):
        zs = slice_at(d, n)
        k_slot = slot_of(d, n)
        partner_wait(d, n)

        def step(k, carry):
            w = w_buf[zs, k].reshape(512, 256)
            w_hi = w.astype(jnp.bfloat16)
            w_lo = (w - w_hi.astype(jnp.float32)).astype(jnp.bfloat16)
            p = jnp.dot(t_hi[k], w_hi, preferred_element_type=jnp.float32)
            p += jnp.dot(t_lo[k], w_hi, preferred_element_type=jnp.float32)
            p += jnp.dot(t_hi[k], w_lo, preferred_element_type=jnp.float32)
            p = p.reshape(8, 2, 32, 256)

            @pl.when(k == 0)
            def _():
                acc[zs] = p

            @pl.when(k > 0)
            def _():
                acc[zs] += p

            return carry

        lax.fori_loop(0, 4, step, 0)
        j = 2 * (xh * NZ + zs) + jj
        lanes = pl.ds(pl.multiple_of(bh * 256, 256), 256)
        dst = out.at[:, j, :, lanes]
        vir_b = vir[:, lanes]
        occ_j = occ[j]
        order = (2, 3, 4, 1, 5, 6, 7, 0)
        for r in order:
            dx, dy = BACK[r]
            xo, yo = (x + dx) % 4, (y + dy) % 4
            column = vir_a[xo // 2]
            column = jnp.concatenate([column, column], axis=1)
            for i in range(2):
                occ_i = occ[(yo * 4 + (xo % 2) * 2 + core) * 2 + i]
                denom = ((occ_i + occ_j) - column) - vir_b
                acc[zs, r, i] = acc[zs, r, i] / denom
        for r in order:
            dx, dy = BACK[r]
            if r > 0:
                start(remote(acc.at[zs, r], dst, c_send.at[r, k_slot], c_recv.at[r, k_slot],
                             place((x + dx) % 4, (y + dy) % 4, z, core)))
            else:
                own = pltpu.make_async_copy(acc.at[zs, r], dst, own_sem.at[k_slot])
                own.start()
                locals_.append(own)

    def relays(n, *chs):
        for ch in chs:
            relay(n, ch)

    def t_ready(*rs):
        for r in rs:
            arrived(t_buf.at[r], t_recv.at[r])
            convert(r)

    relays(0, 0)
    for e in (1, 2, 3, 6, 7, 4, 5):
        start(pre(e))
    send_t(1)
    relays(0, 1, 2, 3, 4)
    send_t(6, 7, 5, 4)
    load_t.wait()
    convert(0)
    relays(1, 0)
    t_ready(1)
    t_relay(2, 1)
    t_relay(3, 3)
    relays(1, 1, 2, 3, 4)
    t_ready(5, 6, 7)
    relays(2, 0, 1, 2)
    t_ready(4, 2, 3)
    relays(2, 3)
    own_w.wait()
    compute(0, 0)
    relays(2, 4)
    compute(0, 1)
    compute(1, 1)
    relays(3, 0)
    compute(0, 2)
    relays(3, 1)
    compute(1, 2)
    relays(3, 2, 3, 4)
    compute(0, 3)
    compute(1, 3)
    relays(4, 0, 1, 3, 2, 4)
    compute(0, 4)

    for cp in pending:
        cp.wait_send()
    for cp in locals_:
        cp.wait()
    for r in range(1, 8):
        for k in range(8):
            arrived(out.at[:, k, :, pl.ds(0, 256)], c_recv.at[r, k])


def body(amplitudes, integrals, occ_energy, vir_energy):
    dma = pltpu.SemaphoreType.DMA
    f32, bf16 = jnp.float32, jnp.bfloat16
    hbm = pl.BlockSpec(memory_space=pltpu.HBM)
    return pl.pallas_call(
        kernel,
        out_shape=jax.ShapeDtypeStruct((2, 32, 32, 512), f32),
        in_specs=[hbm, hbm, pl.BlockSpec(memory_space=pltpu.SMEM), pl.BlockSpec(memory_space=pltpu.VMEM)],
        out_specs=pl.BlockSpec(memory_space=pl.ANY),
        scratch_shapes=[
            pltpu.VMEM((4, 32, 2, 512), f32),
            pltpu.VMEM((2, 2, 4, 32, 256), f32),
            pltpu.VMEM((8, 4, 8, 2, 32, 256), f32),
            pltpu.VMEM((8, 2, 4, 32, 512), f32),
            pltpu.VMEM((4, 512, 512), bf16),
            pltpu.VMEM((4, 512, 512), bf16),
            pltpu.VMEM((8, 8, 2, 32, 256), f32),
            pltpu.VMEM((2, 32, 128), f32),
            dma((3,)), dma((8,)), dma((8,)), dma((2, 4, 5)), dma((2, 4, 5)), dma((8, 5)), dma((8, 5)),
            dma((8,)), dma((8,)), dma((8, 8)), dma((8, 8)), dma((8,)),
        ],
        compiler_params=pltpu.CompilerParams(
            collective_id=0, has_side_effects=True, vmem_limit_bytes=48 * 2**20
        ),
    )(*(pltpu.with_memory_space_constraint(v, pltpu.HBM)
        for v in (amplitudes, integrals, occ_energy, vir_energy.reshape(1, -1))))


def solution(mesh):
    return jax.shard_map(
        body,
        mesh=mesh,
        in_specs=(P("row", None, "col", None), P(None, "row", "col", None), P(), P()),
        out_specs=P("row", None, "col", None),
        check_vma=False,
    )
```

```python
import jax
import jax.numpy as jnp
from jax import lax
from jax.experimental import pallas as pl
from jax.experimental.pallas import tpu as pltpu
from jax.sharding import PartitionSpec as P

MESH = pl.DeviceIdType.MESH
NZ = 8
SHARED_FROM = 2


def place(x, y, z, core):
    return (y * 4 + (x % 2) * 2 + core, (x // 2) * NZ + z)


def flip(v, bits):
    for b in range(3):
        if (bits >> b) & 1:
            v = v + (1 << b) * (1 - 2 * ((v // (1 << b)) % 2))
    return v


def kernel(t_hbm, w_hbm, occ, vir, out, w_raw, w_src, w_buf, t_buf, t_hi, t_lo, acc, vir_a,
           load_sem, pre_send, pre_recv, ring_send, ring_recv, part_send, part_recv,
           swap_send, swap_recv, t_send, t_recv, c_send, c_recv, own_sem):
    row, col = lax.axis_index("row"), lax.axis_index("col")
    y, xl, core = row // 4, (row // 2) % 2, row % 2
    xh, z = col // NZ, col % NZ
    x = xh * 2 + xl
    s = y * 2 + xl
    block = (y + 2 * xl) % 4
    jj, bh = block // 2, block % 2
    inner, outer = 1 + 2 * xl, 3 - 2 * xl
    THERE = ((0, 0), (outer, 0), (outer, 1), (outer, 3), (2, 0), (inner, 0), (0, 1), (0, 3))
    BACK = ((0, 0), (outer, 0), (outer, 3), (outer, 1), (2, 0), (inner, 0), (0, 3), (0, 1))
    z_next = ((z + 1) % NZ, (z + NZ - 1) % NZ)
    partner = place(x, y, z, 1 - core)
    twin = place(xh * 2 + 1 - xl, (y + 2) % 4, z, core)
    pending, locals_ = [], []

    def remote(src, dst, send, recv, device):
        return pltpu.make_async_remote_copy(src, dst, send, recv, device_id=device, device_id_type=MESH)

    def start(cp):
        cp.start()
        pending.append(cp)

    def arrived(view, recv):
        remote(view, view, load_sem.at[0], recv, partner).wait_recv()

    load_w = pltpu.make_async_copy(w_hbm, w_raw, load_sem.at[0])
    load_w.start()
    load_t = pltpu.make_async_copy(t_hbm, t_buf.at[0], load_sem.at[1])
    load_t.start()

    barrier = pltpu.get_barrier_semaphore()
    everyone = [place((x + dx) % 4, (y + dy) % 4, z, core)
                for dx in range(4) for dy in range(4) if (dx, dy) != (0, 0)]
    everyone += [place(x, y, z_next[0], core), place(x, y, z_next[1], core), partner]
    for d in everyone:
        pl.semaphore_signal(barrier, inc=1, device_id=d, device_id_type=MESH)

    load_w.wait()
    for k in range(4):
        for b in range(4):
            w_src[b // 2, b % 2, k] = w_raw[k, :, b // 2, (b % 2) * 256:(b % 2) * 256 + 256]
    pl.semaphore_wait(barrier, len(everyone))

    def pre(e):
        se = flip(s, e)
        ye, xe = se // 2, se % 2
        be = (ye + 2 * xe) % 4
        return remote(w_src.at[be // 2, be % 2], w_buf.at[z, :, s, core], pre_send.at[e], pre_recv.at[e],
                      place(xh * 2 + xe, ye, z, core))

    def pre_wait(e):
        arrived(w_buf.at[z, :, flip(s, e), core], pre_recv.at[e])

    own_w = pltpu.make_async_copy(w_src.at[jj, bh], w_buf.at[z, :, s, core], load_sem.at[2])
    own_w.start()

    def send_t(*rs):
        for r in rs:
            dx, dy = THERE[r]
            start(remote(t_hbm, t_buf.at[r], t_send.at[r], t_recv.at[r],
                         place((x + dx) % 4, (y + dy) % 4, z, core)))

    def t_relay(r, dy):
        start(remote(t_buf.at[1], t_buf.at[r], t_send.at[r], t_recv.at[r], place(x, (y + dy) % 4, z, core)))

    chunks = [(s, 1), (flip(s, 1), 1)] + [((flip(s, e) // 2) * 2, 2) for e in (2, 6, 4)]

    def w_view(zs, ch, which, n):
        base, size = chunks[ch] if ch < 5 else (flip(s, 5), 1)
        if ch == 4 and n >= SHARED_FROM:
            base, size = flip(s, 4), 1
        return w_buf.at[zs, :, pl.ds(base, size), which]

    def slice_at(d, n):
        return (z + NZ - n) % NZ if d == 0 else (z + n) % NZ

    def slot_of(d, n):
        return 0 if n == 0 else 7 if n == 4 else 2 * n - 1 + d

    def goes_on(d, n, ch):
        return n < 3 or (n == 3 and ((ch < 3) if d == 0 else (ch >= 3)))

    def relay(n, ch):
        if n == 0:
            for e in ((), (1,), (2, 3), (6, 7), (4, 5))[ch]:
                pre_wait(e)
        for d in range(2):
            if n == 4 and d != (0 if ch < 3 else 1):
                continue
            v = w_view(slice_at(d, n), ch, core, n)
            if n > 0:
                arrived(v, ring_recv.at[d, n - 1, ch])
            source = v
            if n == 0 and ch == 0:
                source, v = w_src.at[jj, bh], w_buf.at[z, :, s, core]
            k = slot_of(d, n)
            if goes_on(d, n, ch):
                on, to = (source, v)
                if n > 0 or ch == 4:
                    on = to = w_view(slice_at(d, n), ch, core, n + 1)
                start(remote(on, to, ring_send.at[d, n, ch], ring_recv.at[d, n, ch],
                             place(x, y, z_next[d], core)))
            if n >= SHARED_FROM and ch == 0:
                start(remote(v, v, swap_send.at[k], swap_recv.at[k], twin))
            if n > 0 or d == 0:
                start(remote(source, v, part_send.at[k, ch], part_recv.at[k, ch], partner))

    def swapped(n):
        for d in range(2 if n < 4 else 1):
            k = slot_of(d, n)
            v = w_view(slice_at(d, n), 5, core, n)
            arrived(v, swap_recv.at[k])
            start(remote(v, v, part_send.at[k, 5], part_recv.at[k, 5], partner))

    def partner_wait(d, n):
        for ch in range(6 if n >= SHARED_FROM else 5):
            arrived(w_view(slice_at(d, n), ch, 1 - core, n), part_recv.at[slot_of(d, n), ch])

    def pos(r):
        return (r + 7) % 8

    def convert(r):
        for i in range(2):
            for k in range(4):
                v = t_buf[r, i, k]
                hi = v.astype(jnp.bfloat16)
                rows = pl.ds(pos(r) * 64 + i * 32, 32)
                t_hi[k, rows, :] = hi
                t_lo[k, rows, :] = (v - hi.astype(jnp.float32)).astype(jnp.bfloat16)

    lane = lax.broadcasted_iota(jnp.int32, (32, 512), 1)
    sub = lax.broadcasted_iota(jnp.int32, (32, 512), 0)
    vir_row = jnp.broadcast_to(vir[...], (32, 512))
    for h in range(2):
        picked = jnp.where(lane == sub + (h * NZ + z) * 32, vir_row, 0.0)
        vir_a[h] = jnp.broadcast_to(jnp.sum(picked, axis=1, keepdims=True), (32, 128))

    def compute(d, n, groups):
        zs = slice_at(d, n)
        k_slot = slot_of(d, n)
        if 0 in groups:
            partner_wait(d, n)

        j = 2 * (xh * NZ + zs) + jj
        lanes = pl.ds(pl.multiple_of(bh * 256, 256), 256)
        dst = out.at[:, j, :, lanes]
        vir_b = vir[:, lanes]
        occ_j = occ[j]
        for rs in [((1, 2, 3, 4), (5, 6, 7, 0))[g] for g in groups]:
            p0, np_ = pos(rs[0]), len(rs)

            def step(k, carry):
                w = w_buf[zs, k].reshape(512, 256)
                w_hi = w.astype(jnp.bfloat16)
                w_lo = (w - w_hi.astype(jnp.float32)).astype(jnp.bfloat16)
                hi, lo = t_hi[k, p0 * 64:(p0 + np_) * 64, :], t_lo[k, p0 * 64:(p0 + np_) * 64, :]
                p = jnp.dot(hi, w_hi, preferred_element_type=jnp.float32)
                p += jnp.dot(lo, w_hi, preferred_element_type=jnp.float32)
                p += jnp.dot(hi, w_lo, preferred_element_type=jnp.float32)
                p = p.reshape(np_, 2, 32, 256)

                @pl.when(k == 0)
                def _():
                    acc[zs, p0:p0 + np_] = p

                @pl.when(k > 0)
                def _():
                    acc[zs, p0:p0 + np_] += p

                return carry

            lax.fori_loop(0, 4, step, 0)
            order = [r for r in (2, 3, 4, 1, 5, 6, 7, 0) if r in rs]
            for r in order:
                dx, dy = BACK[r]
                xo, yo = (x + dx) % 4, (y + dy) % 4
                column = vir_a[xo // 2]
                column = jnp.concatenate([column, column], axis=1)
                for i in range(2):
                    occ_i = occ[(yo * 4 + (xo % 2) * 2 + core) * 2 + i]
                    denom = ((occ_i + occ_j) - column) - vir_b
                    acc[zs, pos(r), i] = acc[zs, pos(r), i] / denom
            for r in order:
                dx, dy = BACK[r]
                if r > 0:
                    start(remote(acc.at[zs, pos(r)], dst, c_send.at[r, k_slot], c_recv.at[r, k_slot],
                                 place((x + dx) % 4, (y + dy) % 4, z, core)))
                else:
                    own = pltpu.make_async_copy(acc.at[zs, pos(r)], dst, own_sem.at[k_slot])
                    own.start()
                    locals_.append(own)

    def relays(n, *chs):
        for ch in chs:
            relay(n, ch)

    def t_ready(*rs):
        for r in rs:
            arrived(t_buf.at[r], t_recv.at[r])
            convert(r)

    relays(0, 0)
    for e in (1, 2, 3, 6, 7, 4, 5):
        start(pre(e))
    send_t(1, 4)
    relays(0, 1, 2, 3, 4)
    t_ready(1)
    t_relay(2, 1)
    t_relay(3, 3)
    send_t(6, 7, 5)
    load_t.wait()
    convert(0)
    relays(1, 0, 1, 2, 3)
    t_ready(4, 2, 3)
    relays(1, 4)
    own_w.wait()
    compute(0, 0, (0,))
    compute(0, 1, (0,))
    compute(1, 1, (0,))
    relays(2, 0, 1)
    t_ready(5, 6, 7)
    compute(0, 0, (1,))
    relays(2, 2)
    compute(0, 1, (1,))
    relays(2, 3)
    compute(1, 1, (1,))
    swapped(2)
    relays(2, 4)
    compute(0, 2, (0,))
    compute(1, 2, (0,))
    relays(3, 0)
    compute(0, 2, (1,))
    relays(3, 1)
    compute(1, 2, (1,))
    relays(3, 2, 3)
    swapped(3)
    relays(3, 4)
    compute(0, 3, (0,))
    compute(1, 3, (0,))
    compute(0, 3, (1,))
    relays(4, 0, 1, 3)
    compute(1, 3, (1,))
    swapped(4)
    relays(4, 2, 4)
    compute(0, 4, (0, 1))

    for cp in pending:
        cp.wait_send()
    for cp in locals_:
        cp.wait()
    for r in range(1, 8):
        for k in range(8):
            arrived(out.at[:, k, :, pl.ds(0, 256)], c_recv.at[r, k])


def body(amplitudes, integrals, occ_energy, vir_energy):
    dma = pltpu.SemaphoreType.DMA
    f32, bf16 = jnp.float32, jnp.bfloat16
    hbm = pl.BlockSpec(memory_space=pltpu.HBM)
    return pl.pallas_call(
        kernel,
        out_shape=jax.ShapeDtypeStruct((2, 32, 32, 512), f32),
        in_specs=[hbm, hbm, pl.BlockSpec(memory_space=pltpu.SMEM), pl.BlockSpec(memory_space=pltpu.VMEM)],
        out_specs=pl.BlockSpec(memory_space=pl.ANY),
        scratch_shapes=[
            pltpu.VMEM((4, 32, 2, 512), f32),
            pltpu.VMEM((2, 2, 4, 32, 256), f32),
            pltpu.VMEM((8, 4, 8, 2, 32, 256), f32),
            pltpu.VMEM((8, 2, 4, 32, 512), f32),
            pltpu.VMEM((4, 512, 512), bf16),
            pltpu.VMEM((4, 512, 512), bf16),
            pltpu.VMEM((8, 8, 2, 32, 256), f32),
            pltpu.VMEM((2, 32, 128), f32),
            dma((3,)), dma((8,)), dma((8,)), dma((2, 4, 5)), dma((2, 4, 5)), dma((8, 6)), dma((8, 6)), dma((8,)), dma((8,)),
            dma((8,)), dma((8,)), dma((8, 8)), dma((8, 8)), dma((8,)),
        ],
        compiler_params=pltpu.CompilerParams(
            collective_id=0, has_side_effects=True, vmem_limit_bytes=48 * 2**20
        ),
    )(*(pltpu.with_memory_space_constraint(v, pltpu.HBM)
        for v in (amplitudes, integrals, occ_energy, vir_energy.reshape(1, -1))))


def solution(mesh):
    return jax.shard_map(
        body,
        mesh=mesh,
        in_specs=(P("row", None, "col", None), P(None, "row", "col", None), P(), P()),
        out_specs=P("row", None, "col", None),
        check_vma=False,
    )
```
